32 devices in a mesh: tile: 8 (over y, x, core), depth: 4 (over z).
Axes of the slice: x: 2, y: 2, z: 4, core: 2. Of those that a mesh axis runs over, the one named last changes fastest.
Arguments:
- patches: float32 [512, 256, 256], P('tile', 'depth'), may hold values from -6 to 6
- patch_owner: int32 [512, 1], P('tile'), may hold values from 0 to 7; in each aligned block of 64 rows (0 to 63, 64 to 127, ...) at most 8 rows name the same one
- patch_level: int32 [512], P('tile'), may hold values from 0 to 63
- phases: float32 [512, 256, 256], P('tile', None, 'depth'), may hold values from -3.140625 to 3.140625
Outputs:
- intensity: float32 [512, 256, 256], P('tile', 'depth')
The draws below stay inside these ranges and needn't reach their ends.
Inputs may be any that keep to these rules, and one draw needn't show every extreme that they name: `patch_owner`: among the 64 patches of one index of tile, at most 8 have the same owner.
All inputs are finite; a program needn't handle non-finite values.
Results may differ from the reference program's by a relative error of at most 0.00017.
Values sent between devices are 32-bit elements; how exact they have to be, the bound alone decides.
No kernel may reach another device: no remote copies, remote signals or barrier semaphores. Data moves between devices by JAX's collectives and lax.ppermute only.
A program may use at most 128 MiB of HBM per device.

```python
import math
import jax
import jax.numpy as jnp
import numpy as np
from jax import lax

M = 256
P_DEV = 64
CAP = 8
DEP_DEV = 64
OWNERS = 8
DEPTHS = 512
PATCHES = 512


def set_ends(values, rng, smallest, high):
    longest = values.shape.index(max(values.shape))
    spots = []
    for shift in (0, 1):
        where = [jax.random.randint(jax.random.fold_in(rng, axis), (), 0, length) for axis, length in enumerate(values.shape)]
        where[longest] = (where[longest] + shift) % values.shape[longest]
        spots.append(tuple(where))
    return values.at[spots[0]].set(smallest).at[spots[1]].set(high)


def levels(rng, dims, split, smallest, largest):
    level, own = 1.0, jax.random.fold_in(rng, 6)
    for axis_at, shards_of in split:
        heights = jnp.exp(jax.random.uniform(jax.random.fold_in(own, axis_at), (shards_of,), jnp.float32, smallest / len(split), largest / len(split)))
        level = level * jnp.repeat(heights, dims[axis_at] // shards_of).reshape([-1 if axis == axis_at else 1 for axis in range(len(dims))])
    return level


def routed_block(stream_key, own, number, rows, number_of, top, limit, slope):
    ranking = jax.random.permutation(stream_key, number_of)
    packed, common = portions_of(number_of, rows * top, limit, slope, True), portions_of(number_of, rows * top, limit, slope, False)
    places = jnp.arange(number_of)

    def named(lengths, turn):
        used = int((lengths > 0).sum())
        fixed = max(1, used // 4)
        shifted = fixed + (places - fixed + turn * (used - fixed)) % max(1, number_of - fixed)
        return jnp.zeros((number_of,), jnp.int32).at[ranking[jnp.where(places < fixed, places, shifted)]].set(jnp.asarray(lengths, jnp.int32))

    lengths = jnp.where(number % 4 == 0, named(packed, number // 4), named(common, number - number // 4 - 1))
    mixed = jax.random.permutation(jax.random.fold_in(own, 3), number_of)
    donor, taker = mixed[0:number_of // 2 * 2:2], mixed[1:number_of // 2 * 2:2]
    margin = jnp.minimum(lengths[donor] - 1, limit - lengths[taker]) // 2
    margin = jnp.where((donor == ranking[0]) | (taker == ranking[0]) | (lengths[taker] == 0), 0, jnp.maximum(margin, 0))
    shifted = jax.random.randint(jax.random.fold_in(own, 4), (number_of // 2,), 0, 1 << 20) % (margin + 1)
    lengths = lengths.at[donor].add(-shifted).at[taker].add(shifted)
    members = jnp.searchsorted(jnp.cumsum(lengths), jnp.arange(rows * top), side="right").astype(jnp.int32)
    listing = members.reshape(top, rows).T
    listing = listing[jax.random.permutation(jax.random.fold_in(own, 1), rows)]
    turn = jax.random.randint(jax.random.fold_in(own, 2), (rows, 1), 0, top)
    return jnp.take_along_axis(listing, (jnp.arange(top)[None, :] + turn) % top, axis=1)


def portions_of(amount, total, most, lean, full):
    weights = [(1 << 20) // math.isqrt(grade ** lean) + 1 for grade in range(1, amount + 1)]
    largest = most if full else min(most, max(-(-total // amount), total * weights[0] // sum(weights)))
    least = 1 if total - largest >= amount - 1 else 0
    counts, spare = [largest] + [least] * (amount - 1), total - largest - least * (amount - 1)
    while spare > 0:
        movable = [i for i in range(1, amount) if counts[i] < largest] or [i for i in range(1, amount) if counts[i] < most]
        mass, remaining = sum([weights[i] for i in movable]), spare
        for i in movable:
            more = min(most - counts[i], max(1, remaining * weights[i] // mass), spare)
            counts[i] = counts[i] + more
            spare = spare - more
    return np.array(counts)


def centred(key, shape, width, most, cuts=(), dtype=jnp.bfloat16):
    loudness = levels(key, shape, cuts, -0.22, 0.18) if cuts else 1.0
    entries = jax.random.normal(key, shape, jnp.float32) * width * loudness
    return jnp.minimum(jnp.maximum(entries, -most), most).astype(dtype)


def setup_inputs(seed: int = 0) -> dict:
    arg_keys = jax.random.split(jax.random.key(seed), 5)
    patches = centred(arg_keys[0], (PATCHES, M, M), 1.0, 6.0, ((0, 8), (1, 4)), jnp.float32)
    patch_owner_keys = jax.random.split(jax.random.fold_in(arg_keys[1], 1), PATCHES // P_DEV)
    patch_owner_turns = jax.random.permutation(jax.random.fold_in(arg_keys[1], 3), PATCHES // P_DEV)
    patch_owner = jax.vmap(lambda own, number: routed_block(jax.random.fold_in(arg_keys[1], 2), own, number, P_DEV, OWNERS, 1, CAP, 2))(patch_owner_keys, patch_owner_turns).reshape((PATCHES, 1))
    patch_level = set_ends(jax.random.randint(arg_keys[2], (PATCHES,), 0, DEP_DEV), jax.random.fold_in(arg_keys[2], 1), 0, DEP_DEV - 1).astype(jnp.int32)
    phases = jnp.clip(jax.random.uniform(arg_keys[3], (DEPTHS, M, M), jnp.float32, -3.140625, 3.140625), -3.140625, 3.140625)
    return dict(patches=patches, patch_owner=patch_owner, patch_level=patch_level, phases=phases)


def reference(patches, patch_owner, patch_level, phases):
    depth_index = (patch_owner[:, 0] * DEP_DEV + patch_level).astype(jnp.int32)

    def propagate(items):
        patch, chosen = items
        phase = phases[chosen]
        spectrum = jnp.fft.fft2(patch)
        field = jnp.fft.ifft2(spectrum * (jnp.cos(phase) + 1j * jnp.sin(phase)))
        return jnp.real(field) ** 2 + jnp.imag(field) ** 2

    return lax.map(propagate, (patches, depth_index))
```

```python
import functools
import math

import jax
import jax.numpy as jnp
import numpy as np
from jax import lax
from jax.experimental import pallas as pl
from jax.experimental.pallas import tpu as pltpu
from jax.sharding import PartitionSpec as P

CAP = 8


def split(values):
    high = values.astype(jnp.bfloat16)
    low = (values - high.astype(jnp.float32)).astype(jnp.bfloat16)
    return high, low


def tables(extent):
    index = np.arange(extent)
    angles = (index[:, None] * index[None, :] % extent) * (2.0 * math.pi / extent)
    parts = []
    for table in (np.cos(angles), np.sin(angles)):
        table = table.astype(np.float32)
        high = table.astype(jnp.bfloat16)
        parts += [high, (table - high.astype(np.float32)).astype(jnp.bfloat16)]
    return np.stack(parts)


def sincos(angle):
    half = angle * 0.5
    square = half * half
    sine = jnp.float32(-1.0 / math.factorial(11))
    for power, sign in ((9, 1.0), (7, -1.0), (5, 1.0), (3, -1.0), (1, 1.0)):
        sine = sine * square + jnp.float32(sign / math.factorial(power))
    sine = sine * half
    cosine = jnp.float32(1.0 / math.factorial(12))
    for power, sign in ((10, -1.0), (8, 1.0), (6, -1.0), (4, 1.0), (2, -1.0), (0, 1.0)):
        cosine = cosine * square + jnp.float32(sign / math.factorial(power))
    return 2.0 * sine * cosine, 1.0 - 2.0 * sine * sine


def product(left, right, contract):
    dims = (contract, ((), ()))
    dot = functools.partial(
        lax.dot_general, dimension_numbers=dims, preferred_element_type=jnp.float32
    )
    return dot(left[0], right[0]) + (dot(left[0], right[1]) + dot(left[1], right[0]))


NN = ((1,), (0,))
NT = ((1,), (1,))


def refocus_kernel(table_ref, field_ref, phase_ref, out_ref, left_ref, right_ref):
    extent = table_ref.shape[1]

    @pl.when(pl.program_id(0) == 0)
    def _():
        for part in range(2):
            cosine, sine = table_ref[part], table_ref[2 + part]
            left_ref[part, :extent, :extent] = cosine
            left_ref[part, :extent, extent:] = -sine
            left_ref[part, extent:, :extent] = sine
            left_ref[part, extent:, extent:] = cosine
            right_ref[part, :extent, :extent] = cosine
            right_ref[part, :extent, extent:] = sine
            right_ref[part, extent:, :extent] = -sine
            right_ref[part, extent:, extent:] = cosine

    left = (left_ref[0], left_ref[1])
    right = (right_ref[0], right_ref[1])
    patch = field_ref[...].reshape(extent, extent)
    half_turned = product(
        (left_ref[0, :, :extent], left_ref[1, :, :extent]), split(patch), NT
    )
    half_turned = jnp.concatenate([half_turned[:extent], half_turned[extent:]], axis=1)
    spectrum = product(split(half_turned), right, NN)
    spec_real, spec_negated = spectrum[:, :extent], spectrum[:, extent:]
    sine, cosine = sincos(phase_ref[...].reshape(extent, extent))
    prop_real = spec_real * cosine + spec_negated * sine
    prop_imag = spec_real * sine - spec_negated * cosine
    propagated = jnp.concatenate([prop_real, prop_imag], axis=1)
    back = product(left, split(propagated), NT)
    back = jnp.concatenate([back[:extent], back[extent:]], axis=1)
    field = product(split(back), right, NN)
    field_real, field_imag = field[:, :extent], field[:, extent:]
    intensity = (field_real * field_real + field_imag * field_imag) * (1.0 / float(extent) ** 4)
    out_ref[...] = intensity.reshape(out_ref.shape)


def refocus(field, phase, phase_slot_first):
    parts, slots, rows, extent = field.shape
    if phase_slot_first:
        phase_block, phase_map = (1,) + phase.shape[1:], lambda i: (i, 0, 0, 0)
    else:
        phase_block, phase_map = phase.shape[:1] + (1,) + phase.shape[2:], lambda i: (0, i, 0, 0)
    field_spec = pl.BlockSpec((parts, 1, rows, extent), lambda i: (0, i, 0, 0))
    return pl.pallas_call(
        refocus_kernel,
        grid=(slots,),
        in_specs=[
            pl.BlockSpec((4, extent, extent), lambda i: (0, 0, 0)),
            field_spec,
            pl.BlockSpec(phase_block, phase_map),
        ],
        out_specs=field_spec,
        out_shape=jax.ShapeDtypeStruct(field.shape, jnp.float32),
        scratch_shapes=[pltpu.VMEM((2, 2 * extent, 2 * extent), jnp.bfloat16)] * 2,
        name="refocus",
    )(jnp.asarray(tables(extent)), field, phase)


def gather_kernel(index_ref, source_ref, out_ref, sems):
    count = out_ref.shape[0]

    def copy(i):
        return pltpu.make_async_copy(source_ref.at[index_ref[i]], out_ref.at[i], sems.at[i])

    def start(i, _):
        copy(i).start()
        return _

    def wait(i, _):
        copy(i).wait()
        return _

    lax.fori_loop(0, count, start, 0)
    lax.fori_loop(0, count, wait, 0)


def gather(index, source):
    count = index.shape[0]
    return pl.pallas_call(
        gather_kernel,
        grid_spec=pltpu.PrefetchScalarGridSpec(
            num_scalar_prefetch=1,
            in_specs=[pl.BlockSpec(memory_space=pl.ANY)],
            out_specs=pl.BlockSpec(memory_space=pl.ANY),
            scratch_shapes=[pltpu.SemaphoreType.DMA((count,))],
        ),
        out_shape=jax.ShapeDtypeStruct((count,) + source.shape[1:], source.dtype),
        name="gather_blocks",
    )(index, source)


def scatter_kernel(filled, *refs):
    index_ref, source_ref, out_ref, sems = refs[0], refs[1], refs[-2], refs[-1]
    count = source_ref.shape[0]

    def each(act):
        def step(i, _):
            place = index_ref[i]
            if filled:
                act(pltpu.make_async_copy(source_ref.at[i], out_ref.at[place], sems.at[i]))
            else:
                @pl.when(place >= 0)
                def _():
                    act(pltpu.make_async_copy(source_ref.at[i], out_ref.at[place], sems.at[i]))
            return 0

        lax.fori_loop(0, count, step, 0)

    each(lambda copy: copy.start())
    each(lambda copy: copy.wait())


def scatter(index, source, into, out_shape, filled):
    count = source.shape[0]
    anywhere = pl.BlockSpec(memory_space=pl.ANY)
    operands = (source,) if into is None else (source, into)
    return pl.pallas_call(
        functools.partial(scatter_kernel, filled),
        grid_spec=pltpu.PrefetchScalarGridSpec(
            num_scalar_prefetch=1,
            in_specs=[anywhere] * len(operands),
            out_specs=anywhere,
            scratch_shapes=[pltpu.SemaphoreType.DMA((count,))],
        ),
        out_shape=jax.ShapeDtypeStruct(out_shape, source.dtype),
        input_output_aliases={} if into is None else {2: 0},
        name="scatter_blocks",
    )(index, *operands)


def on_device(patches, patch_owner, patch_level, phases):
    patch_count, row_count, extent = patches.shape
    owners = lax.axis_size("tile")
    parts = lax.axis_size("depth")
    slot_count = owners * CAP
    filled = slot_count == patch_count
    direct = CAP % parts == 0
    owner = patch_owner[:, 0]
    numbers = jnp.arange(patch_count, dtype=jnp.int32)
    rank = jnp.sum(
        (owner[:, None] == owner[None, :]) & (numbers[None, :] < numbers[:, None]),
        axis=1,
        dtype=jnp.int32,
    )
    slot = owner * CAP + rank
    slot_hot = jnp.arange(slot_count, dtype=jnp.int32)[:, None] == slot[None, :]
    level_of_slot = jnp.sum(jnp.where(slot_hot, patch_level[None, :], 0), axis=1, dtype=jnp.int32)
    patch_of_slot = jnp.sum(jnp.where(slot_hot, numbers[None, :] + 1, 0), axis=1, dtype=jnp.int32) - 1
    wanted = lax.all_to_all(
        level_of_slot.reshape(owners, CAP), "tile", split_axis=0, concat_axis=0, tiled=True
    )
    turned = jnp.transpose(phases, (0, 2, 1))
    columns = turned.shape[1]
    chunks = CAP // parts if direct else 1
    result = None
    for chunk in range(chunks):
        if direct:
            order = patch_of_slot.reshape(owners, parts, chunks)[:, :, chunk].T.reshape(-1)
            levels = wanted.reshape(owners, parts, chunks)[:, :, chunk].reshape(-1)
        else:
            order, levels = patch_of_slot, wanted.reshape(-1)
        sent = gather(order if filled else jnp.maximum(order, 0), patches)
        field = lax.all_to_all(sent, "depth", split_axis=0, concat_axis=0, tiled=True)
        field = field.reshape(parts, -1, row_count, extent)
        picked = gather(levels, turned)
        if direct:
            phase = lax.all_to_all(
                picked, ("tile", "depth"), split_axis=0, concat_axis=0, tiled=True
            ).reshape(owners, parts, columns, extent)
        else:
            picked = lax.all_to_all(picked, "tile", split_axis=0, concat_axis=0, tiled=True)
            phase = lax.all_to_all(
                picked, "depth", split_axis=0, concat_axis=0, tiled=True
            ).reshape(parts, -1, columns, extent)
        local = refocus(field, phase, direct)
        back = lax.all_to_all(
            local.reshape(-1, row_count, extent), "depth", split_axis=0, concat_axis=0, tiled=True
        )
        result = scatter(order, back, result, patches.shape, filled)
    return result


def solution(mesh):
    return jax.shard_map(
        on_device,
        mesh=mesh,
        in_specs=(P("tile", "depth", None), P("tile", None), P("tile"), P("tile", None, "depth")),
        out_specs=P("tile", "depth", None),
        check_vma=False,
    )
```

```python
import functools
import math

import jax
import jax.numpy as jnp
import numpy as np
from jax import lax
from jax.experimental import pallas as pl
from jax.experimental.pallas import tpu as pltpu
from jax.sharding import PartitionSpec as P

CAP = 8


def split(values):
    high = values.astype(jnp.bfloat16)
    low = (values - high.astype(jnp.float32)).astype(jnp.bfloat16)
    return high, low


def tables(extent):
    index = np.arange(extent)
    angles = (index[:, None] * index[None, :] % extent) * (2.0 * math.pi / extent)
    parts = []
    for table in (np.cos(angles), np.sin(angles)):
        table = table.astype(np.float32)
        high = table.astype(jnp.bfloat16)
        parts += [high, (table - high.astype(np.float32)).astype(jnp.bfloat16)]
    return np.stack(parts)


def sincos(angle):
    half = angle * 0.5
    square = half * half
    sine = jnp.float32(-1.0 / math.factorial(11))
    for power, sign in ((9, 1.0), (7, -1.0), (5, 1.0), (3, -1.0), (1, 1.0)):
        sine = sine * square + jnp.float32(sign / math.factorial(power))
    sine = sine * half
    cosine = jnp.float32(1.0 / math.factorial(12))
    for power, sign in ((10, -1.0), (8, 1.0), (6, -1.0), (4, 1.0), (2, -1.0), (0, 1.0)):
        cosine = cosine * square + jnp.float32(sign / math.factorial(power))
    return 2.0 * sine * cosine, 1.0 - 2.0 * sine * sine


def product(left, right, contract):
    dims = (contract, ((), ()))
    dot = functools.partial(
        lax.dot_general, dimension_numbers=dims, preferred_element_type=jnp.float32
    )
    return dot(left[0], right[0]) + (dot(left[0], right[1]) + dot(left[1], right[0]))


NN = ((1,), (0,))
NT = ((1,), (1,))


def refocus_kernel(table_ref, field_ref, phase_ref, out_ref, left_ref, right_ref):
    extent = table_ref.shape[1]

    @pl.when(pl.program_id(0) == 0)
    def _():
        for part in range(2):
            cosine, sine = table_ref[part], table_ref[2 + part]
            left_ref[part, :extent, :extent] = cosine
            left_ref[part, :extent, extent:] = -sine
            left_ref[part, extent:, :extent] = sine
            left_ref[part, extent:, extent:] = cosine
            right_ref[part, :extent, :extent] = cosine
            right_ref[part, :extent, extent:] = sine
            right_ref[part, extent:, :extent] = -sine
            right_ref[part, extent:, extent:] = cosine

    left = (left_ref[0], left_ref[1])
    right = (right_ref[0], right_ref[1])
    patch = field_ref[...].reshape(extent, extent)
    half_turned = product(
        (left_ref[0, :, :extent], left_ref[1, :, :extent]), split(patch), NT
    )
    half_turned = jnp.concatenate([half_turned[:extent], half_turned[extent:]], axis=1)
    spectrum = product(split(half_turned), right, NN)
    spec_real, spec_negated = spectrum[:, :extent], spectrum[:, extent:]
    sine, cosine = sincos(phase_ref[...].reshape(extent, extent))
    prop_real = spec_real * cosine + spec_negated * sine
    prop_imag = spec_real * sine - spec_negated * cosine
    propagated = jnp.concatenate([prop_real, prop_imag], axis=1)
    back = product(left, split(propagated), NT)
    back = jnp.concatenate([back[:extent], back[extent:]], axis=1)
    field = product(split(back), right, NN)
    field_real, field_imag = field[:, :extent], field[:, extent:]
    intensity = (field_real * field_real + field_imag * field_imag) * (1.0 / float(extent) ** 4)
    out_ref[...] = intensity.reshape(out_ref.shape)


def refocus(field, phase, phase_slot_first):
    parts, slots, rows, extent = field.shape
    if phase_slot_first:
        phase_block, phase_map = (1,) + phase.shape[1:], lambda i: (i, 0, 0, 0)
    else:
        phase_block, phase_map = phase.shape[:1] + (1,) + phase.shape[2:], lambda i: (0, i, 0, 0)
    field_spec = pl.BlockSpec((parts, 1, rows, extent), lambda i: (0, i, 0, 0))
    return pl.pallas_call(
        refocus_kernel,
        grid=(slots,),
        in_specs=[
            pl.BlockSpec((4, extent, extent), lambda i: (0, 0, 0)),
            field_spec,
            pl.BlockSpec(phase_block, phase_map),
        ],
        out_specs=field_spec,
        out_shape=jax.ShapeDtypeStruct(field.shape, jnp.float32),
        scratch_shapes=[pltpu.VMEM((2, 2 * extent, 2 * extent), jnp.bfloat16)] * 2,
        name="refocus",
    )(jnp.asarray(tables(extent)), field, phase)


def move_kernel(scatter, filled, *refs):
    index_ref, source_ref, out_ref, held, come, gone = refs[0], refs[1], *refs[-4:]
    count = held.shape[0]

    def guarded(place, act):
        if filled:
            act()
        else:
            pl.when(place >= 0)(act)

    def each(act):
        def step(i, carry):
            guarded(index_ref[i], lambda: act(i))
            return carry

        lax.fori_loop(0, count, step, 0)

    def fetch(i):
        block = source_ref.at[i if scatter else index_ref[i]]
        return pltpu.make_async_copy(block, held.at[i], come.at[i])

    def store(i):
        block = out_ref.at[index_ref[i] if scatter else i]
        return pltpu.make_async_copy(held.at[i], block, gone.at[i])

    def pass_on(i):
        fetch(i).wait()
        store(i).start()

    each(lambda i: fetch(i).start())
    each(pass_on)
    each(lambda i: store(i).wait())


def move(index, source, out_shape, scatter, filled, into=None):
    count = index.shape[0]
    anywhere = pl.BlockSpec(memory_space=pl.ANY)
    operands = (source,) if into is None else (source, into)
    return pl.pallas_call(
        functools.partial(move_kernel, scatter, filled),
        grid_spec=pltpu.PrefetchScalarGridSpec(
            num_scalar_prefetch=1,
            in_specs=[anywhere] * len(operands),
            out_specs=anywhere,
            scratch_shapes=[
                pltpu.VMEM((count,) + source.shape[1:], source.dtype),
                pltpu.SemaphoreType.DMA((count,)),
                pltpu.SemaphoreType.DMA((count,)),
            ],
        ),
        out_shape=jax.ShapeDtypeStruct(out_shape, source.dtype),
        input_output_aliases={} if into is None else {2: 0},
        name="scatter_blocks" if scatter else "gather_blocks",
    )(index, *operands)


def gather(index, source, filled):
    return move(index, source, index.shape + source.shape[1:], False, filled)


def on_device(patches, patch_owner, patch_level, phases):
    patch_count, row_count, extent = patches.shape
    owners = lax.axis_size("tile")
    parts = lax.axis_size("depth")
    slot_count = owners * CAP
    filled = slot_count == patch_count
    direct = CAP % parts == 0
    owner = patch_owner[:, 0]
    numbers = jnp.arange(patch_count, dtype=jnp.int32)
    rank = jnp.sum(
        (owner[:, None] == owner[None, :]) & (numbers[None, :] < numbers[:, None]),
        axis=1,
        dtype=jnp.int32,
    )
    slot = owner * CAP + rank
    slot_hot = jnp.arange(slot_count, dtype=jnp.int32)[:, None] == slot[None, :]
    level_of_slot = jnp.sum(jnp.where(slot_hot, patch_level[None, :], 0), axis=1, dtype=jnp.int32)
    patch_of_slot = jnp.sum(jnp.where(slot_hot, numbers[None, :] + 1, 0), axis=1, dtype=jnp.int32) - 1
    wanted = lax.all_to_all(
        level_of_slot.reshape(owners, CAP), "tile", split_axis=0, concat_axis=0, tiled=True
    )
    turned = jnp.transpose(phases, (0, 2, 1))
    columns = turned.shape[1]
    chunks = CAP // parts if direct else 1
    result = None
    for chunk in range(chunks):
        if direct:
            order = patch_of_slot.reshape(owners, parts, chunks)[:, :, chunk].T.reshape(-1)
            levels = wanted.reshape(owners, parts, chunks)[:, :, chunk].reshape(-1)
        else:
            order, levels = patch_of_slot, wanted.reshape(-1)
        sent = gather(order, patches, filled)
        field = lax.all_to_all(sent, "depth", split_axis=0, concat_axis=0, tiled=True)
        field = field.reshape(parts, -1, row_count, extent)
        picked = gather(levels, turned, True)
        if direct:
            phase = lax.all_to_all(
                picked, ("tile", "depth"), split_axis=0, concat_axis=0, tiled=True
            ).reshape(owners, parts, columns, extent)
        else:
            picked = lax.all_to_all(picked, "tile", split_axis=0, concat_axis=0, tiled=True)
            phase = lax.all_to_all(
                picked, "depth", split_axis=0, concat_axis=0, tiled=True
            ).reshape(parts, -1, columns, extent)
        local = refocus(field, phase, direct)
        back = lax.all_to_all(
            local.reshape(-1, row_count, extent), "depth", split_axis=0, concat_axis=0, tiled=True
        )
        result = move(order, back, patches.shape, True, filled, result)
    return result


def solution(mesh):
    return jax.shard_map(
        on_device,
        mesh=mesh,
        in_specs=(P("tile", "depth", None), P("tile", None), P("tile"), P("tile", None, "depth")),
        out_specs=P("tile", "depth", None),
        check_vma=False,
    )
```

```python
import functools
import math

import jax
import jax.numpy as jnp
import numpy as np
from jax import lax
from jax.experimental import pallas as pl
from jax.experimental.pallas import tpu as pltpu
from jax.sharding import PartitionSpec as P


CAP = 8


def split(values):
    high = values.astype(jnp.bfloat16)
    low = (values - high.astype(jnp.float32)).astype(jnp.bfloat16)
    return high, low


def tables(extent):
    index = np.arange(extent)
    angles = (index[:, None] * index[None, :] % extent) * (2.0 * math.pi / extent)
    parts = []
    for table in (np.cos(angles), np.sin(angles)):
        table = table.astype(np.float32)
        high = table.astype(jnp.bfloat16)
        parts += [high, (table - high.astype(np.float32)).astype(jnp.bfloat16)]
    return np.stack(parts)


def sincos(angle):
    half = angle * 0.5
    square = half * half
    sine = jnp.float32(-1.0 / math.factorial(11))
    for power, sign in ((9, 1.0), (7, -1.0), (5, 1.0), (3, -1.0), (1, 1.0)):
        sine = sine * square + jnp.float32(sign / math.factorial(power))
    sine = sine * half
    cosine = jnp.float32(1.0 / math.factorial(12))
    for power, sign in ((10, -1.0), (8, 1.0), (6, -1.0), (4, 1.0), (2, -1.0), (0, 1.0)):
        cosine = cosine * square + jnp.float32(sign / math.factorial(power))
    return 2.0 * sine * cosine, 1.0 - 2.0 * sine * sine


def product(left, right, contract):
    dims = (contract, ((), ()))
    dot = functools.partial(
        lax.dot_general, dimension_numbers=dims, preferred_element_type=jnp.float32
    )
    return dot(left[0], right[0]) + (dot(left[0], right[1]) + dot(left[1], right[0]))


NN = ((1,), (0,))
NT = ((1,), (1,))


def rotated(step, parts, rows):
    part = lax.rem(lax.axis_index("depth") + (step + parts), parts)
    return pl.ds(pl.multiple_of(part * rows, rows), rows)


def refocus_kernel(pieces, table_ref, *refs):
    field_refs, phase_ref, out_refs = refs[:pieces], refs[pieces], refs[pieces + 1 : 2 * pieces + 1]
    left_ref, right_ref, whole_ref = refs[2 * pieces + 1 :]
    extent = table_ref.shape[1]

    @pl.when(pl.program_id(0) == 0)
    def _():
        for part in range(2):
            cosine, sine = table_ref[part], table_ref[2 + part]
            left_ref[part, :extent, :extent] = cosine
            left_ref[part, :extent, extent:] = -sine
            left_ref[part, extent:, :extent] = sine
            left_ref[part, extent:, extent:] = cosine
            right_ref[part, :extent, :extent] = cosine
            right_ref[part, :extent, extent:] = sine
            right_ref[part, extent:, :extent] = -sine
            right_ref[part, extent:, extent:] = cosine

    left = (left_ref[0], left_ref[1])
    right = (right_ref[0], right_ref[1])
    if pieces == 1:
        patch = field_refs[0][...].reshape(extent, extent)
    else:
        for step, ref in enumerate(field_refs):
            whole_ref[rotated(-step, pieces, ref.shape[1]), :] = ref[0]
        patch = whole_ref[...]
    half_turned = product(
        (left_ref[0, :, :extent], left_ref[1, :, :extent]), split(patch), NT
    )
    half_turned = jnp.concatenate([half_turned[:extent], half_turned[extent:]], axis=1)
    spectrum = product(split(half_turned), right, NN)
    spec_real, spec_negated = spectrum[:, :extent], spectrum[:, extent:]
    sine, cosine = sincos(phase_ref[...].reshape(extent, extent))
    prop_real = spec_real * cosine + spec_negated * sine
    prop_imag = spec_real * sine - spec_negated * cosine
    propagated = jnp.concatenate([prop_real, prop_imag], axis=1)
    back = product(left, split(propagated), NT)
    back = jnp.concatenate([back[:extent], back[extent:]], axis=1)
    field = product(split(back), right, NN)
    field_real, field_imag = field[:, :extent], field[:, extent:]
    intensity = (field_real * field_real + field_imag * field_imag) * (1.0 / float(extent) ** 4)
    if pieces == 1:
        out_refs[0][...] = intensity.reshape(out_refs[0].shape)
    else:
        whole_ref[...] = intensity
        for step, ref in enumerate(out_refs):
            ref[0] = whole_ref[rotated(step, pieces, ref.shape[1]), :]


def refocus(fields, phase):
    pieces, extent = len(fields), phase.shape[-1]
    if pieces == 1:
        parts, slots, rows, _ = fields[0].shape
        field_spec = pl.BlockSpec((parts, 1, rows, extent), lambda i: (0, i, 0, 0))
        phase_spec = pl.BlockSpec((parts, 1) + phase.shape[2:], lambda i: (0, i, 0, 0))
    else:
        slots, rows, _ = fields[0].shape
        field_spec = pl.BlockSpec((1, rows, extent), lambda i: (i, 0, 0))
        phase_spec = pl.BlockSpec((1,) + phase.shape[1:], lambda i: (i, 0, 0, 0))
    return pl.pallas_call(
        functools.partial(refocus_kernel, pieces),
        grid=(slots,),
        in_specs=[pl.BlockSpec((4, extent, extent), lambda i: (0, 0, 0))]
        + [field_spec] * pieces
        + [phase_spec],
        out_specs=[field_spec] * pieces,
        out_shape=[jax.ShapeDtypeStruct(fields[0].shape, jnp.float32)] * pieces,
        scratch_shapes=[pltpu.VMEM((2, 2 * extent, 2 * extent), jnp.bfloat16)] * 2
        + [pltpu.VMEM((extent, extent), jnp.float32)],
        name="refocus",
    )(jnp.asarray(tables(extent)), *fields, phase)


def move_kernel(scatter, filled, *refs):
    index_ref, source_ref, out_ref, held, come, gone = refs[0], refs[1], *refs[-4:]
    count = held.shape[0]

    def guarded(place, act):
        if filled:
            act()
        else:
            pl.when(place >= 0)(act)

    def each(act):
        def step(i, carry):
            guarded(index_ref[i], lambda: act(i))
            return carry

        lax.fori_loop(0, count, step, 0)

    def fetch(i):
        block = source_ref.at[i if scatter else index_ref[i]]
        return pltpu.make_async_copy(block, held.at[i], come.at[i])

    def store(i):
        block = out_ref.at[index_ref[i] if scatter else i]
        return pltpu.make_async_copy(held.at[i], block, gone.at[i])

    def pass_on(i):
        fetch(i).wait()
        store(i).start()

    each(lambda i: fetch(i).start())
    each(pass_on)
    each(lambda i: store(i).wait())


def move(index, source, out_shape, scatter, filled, into=None):
    count = index.shape[0]
    anywhere = pl.BlockSpec(memory_space=pl.ANY)
    operands = (source,) if into is None else (source, into)
    return pl.pallas_call(
        functools.partial(move_kernel, scatter, filled),
        grid_spec=pltpu.PrefetchScalarGridSpec(
            num_scalar_prefetch=1,
            in_specs=[anywhere] * len(operands),
            out_specs=anywhere,
            scratch_shapes=[
                pltpu.VMEM((count,) + source.shape[1:], source.dtype),
                pltpu.SemaphoreType.DMA((count,)),
                pltpu.SemaphoreType.DMA((count,)),
            ],
        ),
        out_shape=jax.ShapeDtypeStruct(out_shape, source.dtype),
        input_output_aliases={} if into is None else {2: 0},
        name="scatter_blocks" if scatter else "gather_blocks",
    )(index, *operands)


def loop(count, act):
    def step(i, carry):
        act(i)
        return carry

    lax.fori_loop(0, count, step, 0)


def guard(always, condition, act):
    if always:
        act()
    else:
        pl.when(condition)(act)


def step_of(part, parts):
    return lax.rem(part - lax.axis_index("depth") + parts, parts)


def route_kernel(filled, parts, owner_ref, level_ref, patches_ref, order_ref, wanted_ref, *refs):
    out_refs, (held, taken, come, gone) = refs[:parts], refs[parts:]
    owners = held.shape[1]
    slot_count = order_ref.shape[0]
    per_owner = slot_count // owners

    def clear(i):
        taken[i] = 0

    loop(owners, clear)
    if not filled:

        def empty(i):
            order_ref[i] = -1
            wanted_ref[i] = 0

        loop(slot_count, empty)

    def place(i):
        owner = owner_ref[i]
        rank = taken[owner]
        taken[owner] = rank + 1
        slot = owner * per_owner + rank
        order_ref[slot] = i
        wanted_ref[slot] = level_ref[i]

        @pl.when(rank < parts)
        def _():
            step = step_of(rank, parts)
            pltpu.make_async_copy(
                patches_ref.at[i], held.at[step, owner], come.at[step, owner]
            ).start()

    loop(owner_ref.shape[0], place)
    send_on(filled, 0, order_ref, patches_ref, out_refs, held, come, gone)


def send_on(filled, chunk, order_ref, patches_ref, out_refs, held, come, gone):
    parts, owners = held.shape[:2]
    per_owner = order_ref.shape[0] // owners

    def slot_patch(step, owner):
        part = lax.rem(lax.axis_index("depth") + step, parts)
        return order_ref[owner * per_owner + chunk * parts + part]

    for step in [*range(1, parts), 0]:

        def pass_on(owner):
            def act():
                pltpu.make_async_copy(
                    patches_ref.at[0], held.at[step, owner], come.at[step, owner]
                ).wait()

            guard(filled, slot_patch(step, owner) >= 0, act)
            pltpu.make_async_copy(
                held.at[step, owner], out_refs[step].at[owner], gone.at[step, owner]
            ).start()

        loop(owners, pass_on)
    for step in range(parts):
        loop(
            owners,
            lambda owner: pltpu.make_async_copy(
                held.at[step, owner], out_refs[step].at[owner], gone.at[step, owner]
            ).wait(),
        )


def scratch_of(parts, owners, block):
    return [
        pltpu.VMEM((parts, owners) + block, jnp.float32),
        pltpu.SemaphoreType.DMA((parts, owners)),
        pltpu.SemaphoreType.DMA((parts, owners)),
    ]


ANYWHERE = pl.BlockSpec(memory_space=pl.ANY)
SCALARS = pl.BlockSpec(memory_space=pltpu.SMEM)


def route(owner, level, patches, owners, parts, slot_count, filled):
    block = patches.shape[1:]
    held, come, gone = scratch_of(parts, owners, block)
    return pl.pallas_call(
        functools.partial(route_kernel, filled, parts),
        in_specs=[SCALARS, SCALARS, ANYWHERE],
        out_specs=[SCALARS, SCALARS] + [ANYWHERE] * parts,
        out_shape=[jax.ShapeDtypeStruct((slot_count,), jnp.int32)] * 2
        + [jax.ShapeDtypeStruct((owners,) + block, patches.dtype)] * parts,
        scratch_shapes=[held, pltpu.SMEM((owners,), jnp.int32), come, gone],
        name="route",
    )(owner, level, patches)


def chunk_kernel(filled, chunk, order_ref, patches_ref, *refs):
    out_refs, (held, come, gone) = refs[-3 - refs[-3].shape[0] : -3], refs[-3:]
    parts, owners = held.shape[:2]
    per_owner = order_ref.shape[0] // owners
    for step in range(parts):

        def fetch(owner):
            part = lax.rem(lax.axis_index("depth") + step, parts)
            number = order_ref[owner * per_owner + chunk * parts + part]

            def act():
                pltpu.make_async_copy(
                    patches_ref.at[number], held.at[step, owner], come.at[step, owner]
                ).start()

            guard(filled, number >= 0, act)

        loop(owners, fetch)
    send_on(filled, chunk, order_ref, patches_ref, out_refs, held, come, gone)


def fetch_chunk(order, patches, owners, parts, chunk, filled):
    block = patches.shape[1:]
    return pl.pallas_call(
        functools.partial(chunk_kernel, filled, chunk),
        in_specs=[SCALARS, ANYWHERE],
        out_specs=[ANYWHERE] * parts,
        out_shape=[jax.ShapeDtypeStruct((owners,) + block, patches.dtype)] * parts,
        scratch_shapes=scratch_of(parts, owners, block),
        name="fetch_chunk",
    )(order, patches)


def store_kernel(filled, chunk, parts, order_ref, *refs):
    source_refs, out_ref, (held, come, gone) = refs[:parts], refs[-4], refs[-3:]
    owners = held.shape[1]
    per_owner = order_ref.shape[0] // owners

    def fetch(step, owner):
        return pltpu.make_async_copy(
            source_refs[step].at[owner], held.at[step, owner], come.at[step, owner]
        )

    def store(step, owner, number):
        return pltpu.make_async_copy(
            held.at[step, owner], out_ref.at[number], gone.at[step, owner]
        )

    def each(act):
        for step in range(parts):

            def one(owner):
                part = lax.rem(lax.axis_index("depth") + (parts - step), parts)
                number = order_ref[owner * per_owner + chunk * parts + part]
                guard(filled, number >= 0, lambda: act(step, owner, number))

            loop(owners, one)

    def pass_on(step, owner, number):
        fetch(step, owner).wait()
        store(step, owner, number).start()

    each(lambda step, owner, number: fetch(step, owner).start())
    each(pass_on)
    each(lambda step, owner, number: store(step, owner, number).wait())


def store_chunk(order, sources, into, out_shape, chunk, filled):
    parts, owners, block = len(sources), sources[0].shape[0], sources[0].shape[1:]
    operands = sources if into is None else sources + [into]
    return pl.pallas_call(
        functools.partial(store_kernel, filled, chunk, parts),
        in_specs=[SCALARS] + [ANYWHERE] * len(operands),
        out_specs=ANYWHERE,
        out_shape=jax.ShapeDtypeStruct(out_shape, jnp.float32),
        scratch_shapes=scratch_of(parts, owners, block),
        input_output_aliases={} if into is None else {len(operands): 0},
        name="store_chunk",
    )(order, *operands)


def pick_kernel(parts, chunk, wanted_ref, source_ref, out_ref, held, come, gone):
    count = held.shape[0]
    per_source = wanted_ref.shape[0] * parts // count

    def fetch(i):
        level = wanted_ref[i // parts * per_source + chunk * parts + lax.rem(i, parts)]
        return pltpu.make_async_copy(source_ref.at[level], held.at[i], come.at[i])

    def store(i):
        return pltpu.make_async_copy(held.at[i], out_ref.at[i], gone.at[i])

    def pass_on(i):
        fetch(i).wait()
        store(i).start()

    loop(count, lambda i: fetch(i).start())
    loop(count, pass_on)
    loop(count, lambda i: store(i).wait())


def pick_phases(wanted, phases, owners, parts, chunk):
    count, block = owners * parts, phases.shape[1:]
    return pl.pallas_call(
        functools.partial(pick_kernel, parts, chunk),
        in_specs=[SCALARS, ANYWHERE],
        out_specs=ANYWHERE,
        out_shape=jax.ShapeDtypeStruct((count,) + block, phases.dtype),
        scratch_shapes=[
            pltpu.VMEM((count,) + block, phases.dtype),
            pltpu.SemaphoreType.DMA((count,)),
            pltpu.SemaphoreType.DMA((count,)),
        ],
        name="pick_phases",
    )(wanted, phases)


def spread(arrays):
    parts = len(arrays)
    return arrays[:1] + [
        lax.ppermute(arrays[step], "depth", [(i, (i + step) % parts) for i in range(parts)])
        for step in range(1, parts)
    ]


def exchange(values, axes):
    return lax.all_to_all(values, axes, split_axis=0, concat_axis=0, tiled=True)


def by_chunks(patches, patch_owner, patch_level, phases):
    patch_count, _, extent = patches.shape
    owners, parts = lax.axis_size("tile"), lax.axis_size("depth")
    slot_count = owners * CAP
    filled = slot_count == patch_count
    columns = phases.shape[1]
    order, wanted, *sent = route(
        patch_owner[:, 0], patch_level, patches, owners, parts, slot_count, filled
    )
    wanted = exchange(wanted.reshape(owners, CAP), "tile").reshape(-1)
    result = None
    for chunk in range(CAP // parts):
        if chunk:
            sent = fetch_chunk(order, patches, owners, parts, chunk, filled)
        fields = spread(list(sent))
        picked = pick_phases(wanted, phases, owners, parts, chunk)
        phase = exchange(picked, ("tile", "depth"))
        local = refocus(fields, phase.reshape(owners, parts, columns, extent))
        backs = spread(list(local))
        result = store_chunk(order, backs, result, patches.shape, chunk, filled)
    return result


def by_owner(patches, patch_owner, patch_level, phases):
    patch_count, row_count, extent = patches.shape
    owners, parts = lax.axis_size("tile"), lax.axis_size("depth")
    slot_count = owners * CAP
    filled = slot_count == patch_count
    owner = patch_owner[:, 0]
    numbers = jnp.arange(patch_count, dtype=jnp.int32)
    rank = jnp.sum(
        (owner[:, None] == owner[None, :]) & (numbers[None, :] < numbers[:, None]),
        axis=1,
        dtype=jnp.int32,
    )
    slot_hot = jnp.arange(slot_count, dtype=jnp.int32)[:, None] == (owner * CAP + rank)[None, :]
    wanted = jnp.sum(jnp.where(slot_hot, patch_level[None, :], 0), axis=1, dtype=jnp.int32)
    order = jnp.sum(jnp.where(slot_hot, numbers[None, :] + 1, 0), axis=1, dtype=jnp.int32) - 1
    wanted = exchange(wanted.reshape(owners, CAP), "tile").reshape(-1)
    field = exchange(move(order, patches, (slot_count,) + patches.shape[1:], False, filled), "depth")
    picked = move(wanted, phases, (slot_count,) + phases.shape[1:], False, True)
    phase = exchange(exchange(picked, "tile"), "depth")
    (local,) = refocus(
        [field.reshape(parts, -1, row_count, extent)],
        phase.reshape((parts, -1) + phases.shape[1:]),
    )
    back = exchange(local.reshape(-1, row_count, extent), "depth")
    return move(order, back, patches.shape, True, filled)


def on_device(patches, patch_owner, patch_level, phases):
    turned = jnp.transpose(phases, (0, 2, 1))
    plan = by_chunks if CAP % lax.axis_size("depth") == 0 else by_owner
    return plan(patches, patch_owner, patch_level, turned)


def solution(mesh):
    return jax.shard_map(
        on_device,
        mesh=mesh,
        in_specs=(P("tile", "depth", None), P("tile", None), P("tile"), P("tile", None, "depth")),
        out_specs=P("tile", "depth", None),
        check_vma=False,
    )
```

```python
import functools
import math

import jax
import jax.numpy as jnp
import numpy as np
from jax import lax
from jax.experimental import pallas as pl
from jax.experimental.pallas import tpu as pltpu
from jax.sharding import PartitionSpec as P


CAP = 8


def split(values):
    high = values.astype(jnp.bfloat16)
    low = (values - high.astype(jnp.float32)).astype(jnp.bfloat16)
    return high, low


def tables(extent):
    index = np.arange(extent)
    angles = (index[:, None] * index[None, :] % extent) * (2.0 * math.pi / extent)
    parts = []
    for table in (np.cos(angles), np.sin(angles)):
        table = table.astype(np.float32)
        high = table.astype(jnp.bfloat16)
        parts += [high, (table - high.astype(np.float32)).astype(jnp.bfloat16)]
    return np.stack(parts)


def sincos(angle):
    half = angle * 0.5
    square = half * half
    sine = jnp.float32(-1.0 / math.factorial(11))
    for power, sign in ((9, 1.0), (7, -1.0), (5, 1.0), (3, -1.0), (1, 1.0)):
        sine = sine * square + jnp.float32(sign / math.factorial(power))
    sine = sine * half
    cosine = jnp.float32(1.0 / math.factorial(12))
    for power, sign in ((10, -1.0), (8, 1.0), (6, -1.0), (4, 1.0), (2, -1.0), (0, 1.0)):
        cosine = cosine * square + jnp.float32(sign / math.factorial(power))
    return 2.0 * sine * cosine, 1.0 - 2.0 * sine * sine


def product(left, right, contract):
    dims = (contract, ((), ()))
    dot = functools.partial(
        lax.dot_general, dimension_numbers=dims, preferred_element_type=jnp.float32
    )
    return dot(left[0], right[0]) + (dot(left[0], right[1]) + dot(left[1], right[0]))


NN = ((1,), (0,))
NT = ((1,), (1,))


def partner(step):
    return lax.bitwise_xor(lax.axis_index("depth"), step)


def rows_with(step, rows):
    return pl.ds(pl.multiple_of(partner(step) * rows, rows), rows)


def refocus_kernel(pieces, table_ref, *refs):
    field_refs, phase_ref, out_refs = refs[:pieces], refs[pieces], refs[pieces + 1 : 2 * pieces + 1]
    left_ref, right_ref, whole_ref = refs[2 * pieces + 1 :]
    extent = table_ref.shape[1]

    @pl.when(pl.program_id(0) == 0)
    def _():
        for part in range(2):
            cosine, sine = table_ref[part], table_ref[2 + part]
            left_ref[part, :extent, :extent] = cosine
            left_ref[part, :extent, extent:] = -sine
            left_ref[part, extent:, :extent] = sine
            left_ref[part, extent:, extent:] = cosine
            right_ref[part, :extent, :extent] = cosine
            right_ref[part, :extent, extent:] = sine
            right_ref[part, extent:, :extent] = -sine
            right_ref[part, extent:, extent:] = cosine

    left = (left_ref[0], left_ref[1])
    right = (right_ref[0], right_ref[1])
    if pieces == 1:
        patch = field_refs[0][...].reshape(extent, extent)
    else:
        for step, ref in enumerate(field_refs):
            whole_ref[rows_with(step, ref.shape[1]), :] = ref[0]
        patch = whole_ref[...]
    half_turned = product(
        (left_ref[0, :, :extent], left_ref[1, :, :extent]), split(patch), NT
    )
    half_turned = jnp.concatenate([half_turned[:extent], half_turned[extent:]], axis=1)
    spectrum = product(split(half_turned), right, NN)
    spec_real, spec_negated = spectrum[:, :extent], spectrum[:, extent:]
    sine, cosine = sincos(phase_ref[...].reshape(extent, extent))
    prop_real = spec_real * cosine + spec_negated * sine
    prop_imag = spec_real * sine - spec_negated * cosine
    propagated = jnp.concatenate([prop_real, prop_imag], axis=1)
    back = product(left, split(propagated), NT)
    back = jnp.concatenate([back[:extent], back[extent:]], axis=1)
    field = product(split(back), right, NN)
    field_real, field_imag = field[:, :extent], field[:, extent:]
    intensity = (field_real * field_real + field_imag * field_imag) * (1.0 / float(extent) ** 4)
    if pieces == 1:
        out_refs[0][...] = intensity.reshape(out_refs[0].shape)
    else:
        whole_ref[...] = intensity
        for step, ref in enumerate(out_refs):
            ref[0] = whole_ref[rows_with(step, ref.shape[1]), :]


def refocus(fields, phase):
    pieces, extent = len(fields), phase.shape[-1]
    fields = [pltpu.with_memory_space_constraint(field, pltpu.HBM) for field in fields]
    phase = pltpu.with_memory_space_constraint(phase, pltpu.HBM)
    if pieces == 1:
        parts, slots, rows, _ = fields[0].shape
        field_spec = pl.BlockSpec((parts, 1, rows, extent), lambda i: (0, i, 0, 0))
        phase_spec = pl.BlockSpec((parts, 1) + phase.shape[2:], lambda i: (0, i, 0, 0))
    else:
        slots, rows, _ = fields[0].shape
        field_spec = pl.BlockSpec((1, rows, extent), lambda i: (i, 0, 0))
        phase_spec = pl.BlockSpec((1,) + phase.shape[1:], lambda i: (i, 0, 0, 0))
    return pl.pallas_call(
        functools.partial(refocus_kernel, pieces),
        grid=(slots,),
        in_specs=[pl.BlockSpec((4, extent, extent), lambda i: (0, 0, 0))]
        + [field_spec] * pieces
        + [phase_spec],
        out_specs=[field_spec] * pieces,
        out_shape=[jax.ShapeDtypeStruct(fields[0].shape, jnp.float32)] * pieces,
        scratch_shapes=[pltpu.VMEM((2, 2 * extent, 2 * extent), jnp.bfloat16)] * 2
        + [pltpu.VMEM((extent, extent), jnp.float32)],
        name="refocus",
    )(jnp.asarray(tables(extent)), *fields, phase)


def move_kernel(scatter, filled, *refs):
    index_ref, source_ref, out_ref, held, come, gone = refs[0], refs[1], *refs[-4:]
    count = held.shape[0]

    def guarded(place, act):
        if filled:
            act()
        else:
            pl.when(place >= 0)(act)

    def each(act):
        def step(i, carry):
            guarded(index_ref[i], lambda: act(i))
            return carry

        lax.fori_loop(0, count, step, 0)

    def fetch(i):
        block = source_ref.at[i if scatter else index_ref[i]]
        return pltpu.make_async_copy(block, held.at[i], come.at[i])

    def store(i):
        block = out_ref.at[index_ref[i] if scatter else i]
        return pltpu.make_async_copy(held.at[i], block, gone.at[i])

    def pass_on(i):
        fetch(i).wait()
        store(i).start()

    each(lambda i: fetch(i).start())
    each(pass_on)
    each(lambda i: store(i).wait())


def move(index, source, out_shape, scatter, filled, into=None):
    count = index.shape[0]
    anywhere = pl.BlockSpec(memory_space=pl.ANY)
    operands = (source,) if into is None else (source, into)
    return pl.pallas_call(
        functools.partial(move_kernel, scatter, filled),
        grid_spec=pltpu.PrefetchScalarGridSpec(
            num_scalar_prefetch=1,
            in_specs=[anywhere] * len(operands),
            out_specs=anywhere,
            scratch_shapes=[
                pltpu.VMEM((count,) + source.shape[1:], source.dtype),
                pltpu.SemaphoreType.DMA((count,)),
                pltpu.SemaphoreType.DMA((count,)),
            ],
        ),
        out_shape=jax.ShapeDtypeStruct(out_shape, source.dtype),
        input_output_aliases={} if into is None else {2: 0},
        name="scatter_blocks" if scatter else "gather_blocks",
    )(index, *operands)


def loop(count, act):
    def step(i, carry):
        act(i)
        return carry

    lax.fori_loop(0, count, step, 0)


def guard(always, condition, act):
    if always:
        act()
    else:
        pl.when(condition)(act)


def route_kernel(filled, parts, owner_ref, level_ref, patches_ref, order_ref, wanted_ref, *refs):
    out_refs, (taken, come) = refs[:parts], refs[parts:]
    owners = out_refs[0].shape[0]
    slot_count = order_ref.shape[0]
    per_owner = slot_count // owners

    def clear(i):
        taken[i] = 0

    loop(owners, clear)
    if not filled:

        def empty(i):
            order_ref[i] = -1
            wanted_ref[i] = 0

        loop(slot_count, empty)

    def place(i):
        owner = owner_ref[i]
        rank = taken[owner]
        taken[owner] = rank + 1
        slot = owner * per_owner + rank
        order_ref[slot] = i
        wanted_ref[slot] = level_ref[i]
        step = partner(rank)
        for at in range(parts):

            @pl.when((rank < parts) & (step == at))
            def _():
                pltpu.make_async_copy(
                    patches_ref.at[i], out_refs[at].at[owner], come.at[at, owner]
                ).start()

    loop(owner_ref.shape[0], place)
    for step in range(parts):

        def arrive(owner):
            def act():
                pltpu.make_async_copy(
                    patches_ref.at[0], out_refs[step].at[owner], come.at[step, owner]
                ).wait()

            guard(filled, order_ref[owner * per_owner + partner(step)] >= 0, act)

        loop(owners, arrive)


def send_on(filled, chunk, order_ref, patches_ref, out_refs, held, come, gone):
    parts, owners = held.shape[:2]
    per_owner = order_ref.shape[0] // owners

    def slot_patch(step, owner):
        return order_ref[owner * per_owner + chunk * parts + partner(step)]

    for step in [*range(1, parts), 0]:

        def pass_on(owner):
            def act():
                pltpu.make_async_copy(
                    patches_ref.at[0], held.at[step, owner], come.at[step, owner]
                ).wait()

            guard(filled, slot_patch(step, owner) >= 0, act)
            pltpu.make_async_copy(
                held.at[step, owner], out_refs[step].at[owner], gone.at[step, owner]
            ).start()

        loop(owners, pass_on)
    for step in range(parts):
        loop(
            owners,
            lambda owner: pltpu.make_async_copy(
                held.at[step, owner], out_refs[step].at[owner], gone.at[step, owner]
            ).wait(),
        )


def scratch_of(parts, owners, block):
    return [
        pltpu.VMEM((parts, owners) + block, jnp.float32),
        pltpu.SemaphoreType.DMA((parts, owners)),
        pltpu.SemaphoreType.DMA((parts, owners)),
    ]


ANYWHERE = pl.BlockSpec(memory_space=pl.ANY)
SCALARS = pl.BlockSpec(memory_space=pltpu.SMEM)


def route(owner, level, patches, owners, parts, slot_count, filled):
    block = patches.shape[1:]
    return pl.pallas_call(
        functools.partial(route_kernel, filled, parts),
        in_specs=[SCALARS, SCALARS, ANYWHERE],
        out_specs=[SCALARS, SCALARS] + [pl.BlockSpec(memory_space=pltpu.VMEM)] * parts,
        out_shape=[jax.ShapeDtypeStruct((slot_count,), jnp.int32)] * 2
        + [jax.ShapeDtypeStruct((owners,) + block, patches.dtype)] * parts,
        scratch_shapes=[
            pltpu.SMEM((owners,), jnp.int32),
            pltpu.SemaphoreType.DMA((parts, owners)),
        ],
        name="route",
    )(owner, level, patches)


def chunk_kernel(filled, chunk, order_ref, patches_ref, *refs):
    out_refs, (held, come, gone) = refs[-3 - refs[-3].shape[0] : -3], refs[-3:]
    parts, owners = held.shape[:2]
    per_owner = order_ref.shape[0] // owners
    for step in range(parts):

        def fetch(owner):
            number = order_ref[owner * per_owner + chunk * parts + partner(step)]

            def act():
                pltpu.make_async_copy(
                    patches_ref.at[number], held.at[step, owner], come.at[step, owner]
                ).start()

            guard(filled, number >= 0, act)

        loop(owners, fetch)
    send_on(filled, chunk, order_ref, patches_ref, out_refs, held, come, gone)


def fetch_chunk(order, patches, owners, parts, chunk, filled):
    block = patches.shape[1:]
    return pl.pallas_call(
        functools.partial(chunk_kernel, filled, chunk),
        in_specs=[SCALARS, ANYWHERE],
        out_specs=[ANYWHERE] * parts,
        out_shape=[jax.ShapeDtypeStruct((owners,) + block, patches.dtype)] * parts,
        scratch_shapes=scratch_of(parts, owners, block),
        name="fetch_chunk",
    )(order, patches)


def store_kernel(filled, chunk, parts, steps, order_ref, *refs):
    source_refs, out_ref, gone = refs[: len(steps)], refs[-2], refs[-1]
    owners = gone.shape[1]
    per_owner = order_ref.shape[0] // owners

    def each(act):
        for at, step in enumerate(steps):

            def one(owner):
                number = order_ref[owner * per_owner + chunk * parts + partner(step)]
                copy = pltpu.make_async_copy(
                    source_refs[at].at[owner], out_ref.at[number], gone.at[at, owner]
                )
                guard(filled, number >= 0, lambda: act(copy))

            loop(owners, one)

    each(lambda copy: copy.start())
    each(lambda copy: copy.wait())


def store_chunk(order, sources, into, out_shape, chunk, parts, steps, filled):
    owners = sources[0].shape[0]
    sources = [pltpu.with_memory_space_constraint(source, pltpu.VMEM) for source in sources]
    operands = sources if into is None else sources + [into]
    return pl.pallas_call(
        functools.partial(store_kernel, filled, chunk, parts, steps),
        in_specs=[SCALARS]
        + [pl.BlockSpec(memory_space=pltpu.VMEM)] * len(sources)
        + [ANYWHERE] * (into is not None),
        out_specs=ANYWHERE,
        out_shape=jax.ShapeDtypeStruct(out_shape, jnp.float32),
        scratch_shapes=[pltpu.SemaphoreType.DMA((len(steps), owners))],
        input_output_aliases={} if into is None else {len(operands): 0},
        name="store_chunk",
    )(order, *operands)


def pick_kernel(parts, chunk, wanted_ref, source_ref, out_ref, held, come, gone):
    count = held.shape[0]
    per_source = wanted_ref.shape[0] * parts // count

    def fetch(i):
        level = wanted_ref[i // parts * per_source + chunk * parts + lax.rem(i, parts)]
        return pltpu.make_async_copy(source_ref.at[level], held.at[i], come.at[i])

    def store(i):
        return pltpu.make_async_copy(held.at[i], out_ref.at[i], gone.at[i])

    def pass_on(i):
        fetch(i).wait()
        store(i).start()

    loop(count, lambda i: fetch(i).start())
    loop(count, pass_on)
    loop(count, lambda i: store(i).wait())


def pick_phases(wanted, phases, owners, parts, chunk):
    count, block = owners * parts, phases.shape[1:]
    return pl.pallas_call(
        functools.partial(pick_kernel, parts, chunk),
        in_specs=[SCALARS, ANYWHERE],
        out_specs=ANYWHERE,
        out_shape=jax.ShapeDtypeStruct((count,) + block, phases.dtype),
        scratch_shapes=[
            pltpu.VMEM((count,) + block, phases.dtype),
            pltpu.SemaphoreType.DMA((count,)),
            pltpu.SemaphoreType.DMA((count,)),
        ],
        name="pick_phases",
    )(wanted, phases)


def swap(arrays):
    parts = len(arrays)
    swapped = list(arrays)
    for step in range(parts - 1, 0, -1):
        swapped[step] = lax.ppermute(
            arrays[step], "depth", [(part, part ^ step) for part in range(parts)]
        )
    return swapped


def exchange(values, axes):
    return lax.all_to_all(values, axes, split_axis=0, concat_axis=0, tiled=True)


def by_chunks(patches, patch_owner, patch_level, phases):
    patch_count, _, extent = patches.shape
    owners, parts = lax.axis_size("tile"), lax.axis_size("depth")
    slot_count = owners * CAP
    filled = slot_count == patch_count
    columns = phases.shape[1]
    order, wanted, *sent = route(
        patch_owner[:, 0], patch_level, patches, owners, parts, slot_count, filled
    )
    wanted = exchange(wanted.reshape(owners, CAP), "tile").reshape(-1)
    result = None
    for chunk in range(CAP // parts):
        if chunk:
            sent = fetch_chunk(order, patches, owners, parts, chunk, filled)
        fields = swap(sent)
        picked = pick_phases(wanted, phases, owners, parts, chunk)
        phase = exchange(picked, ("tile", "depth"))
        local = refocus(fields, phase.reshape(owners, parts, columns, extent))
        backs = swap(local)
        last = chunk == CAP // parts - 1
        every = tuple(range(parts))
        for steps in (every[:1], every[1:2], every[2:]) if last else (every,):
            if not steps:
                continue
            result = store_chunk(
                order,
                [backs[step] for step in steps],
                result,
                patches.shape,
                chunk,
                parts,
                steps,
                filled,
            )
    return result


def by_owner(patches, patch_owner, patch_level, phases):
    patch_count, row_count, extent = patches.shape
    owners, parts = lax.axis_size("tile"), lax.axis_size("depth")
    slot_count = owners * CAP
    filled = slot_count == patch_count
    owner = patch_owner[:, 0]
    numbers = jnp.arange(patch_count, dtype=jnp.int32)
    rank = jnp.sum(
        (owner[:, None] == owner[None, :]) & (numbers[None, :] < numbers[:, None]),
        axis=1,
        dtype=jnp.int32,
    )
    slot_hot = jnp.arange(slot_count, dtype=jnp.int32)[:, None] == (owner * CAP + rank)[None, :]
    wanted = jnp.sum(jnp.where(slot_hot, patch_level[None, :], 0), axis=1, dtype=jnp.int32)
    order = jnp.sum(jnp.where(slot_hot, numbers[None, :] + 1, 0), axis=1, dtype=jnp.int32) - 1
    wanted = exchange(wanted.reshape(owners, CAP), "tile").reshape(-1)
    field = exchange(move(order, patches, (slot_count,) + patches.shape[1:], False, filled), "depth")
    picked = move(wanted, phases, (slot_count,) + phases.shape[1:], False, True)
    phase = exchange(exchange(picked, "tile"), "depth")
    (local,) = refocus(
        [field.reshape(parts, -1, row_count, extent)],
        phase.reshape((parts, -1) + phases.shape[1:]),
    )
    back = exchange(local.reshape(-1, row_count, extent), "depth")
    return move(order, back, patches.shape, True, filled)


def on_device(patches, patch_owner, patch_level, phases):
    turned = jnp.transpose(phases, (0, 2, 1))
    plan = by_chunks if CAP % lax.axis_size("depth") == 0 else by_owner
    return plan(patches, patch_owner, patch_level, turned)


def solution(mesh):
    return jax.shard_map(
        on_device,
        mesh=mesh,
        in_specs=(P("tile", "depth", None), P("tile", None), P("tile"), P("tile", None, "depth")),
        out_specs=P("tile", "depth", None),
        check_vma=False,
    )
```

```python
import functools
import math

import jax
import jax.numpy as jnp
import numpy as np
from jax import lax
from jax.experimental import pallas as pl
from jax.experimental.pallas import tpu as pltpu
from jax.sharding import PartitionSpec as P


CAP = 8
CHUNKS = 2
TOGETHER = 2


def split(values):
    high = values.astype(jnp.bfloat16)
    low = (values - high.astype(jnp.float32)).astype(jnp.bfloat16)
    return high, low


def tables(extent):
    index = np.arange(extent)
    angles = (index[:, None] * index[None, :] % extent) * (2.0 * math.pi / extent)
    parts = []
    for table in (np.cos(angles), np.sin(angles)):
        table = table.astype(np.float32)
        high = table.astype(jnp.bfloat16)
        parts += [high, (table - high.astype(np.float32)).astype(jnp.bfloat16)]
    return np.stack(parts)


def sincos(angle):
    half = angle * 0.5
    square = half * half
    sine = jnp.float32(-1.0 / math.factorial(11))
    for power, sign in ((9, 1.0), (7, -1.0), (5, 1.0), (3, -1.0), (1, 1.0)):
        sine = sine * square + jnp.float32(sign / math.factorial(power))
    sine = sine * half
    cosine = jnp.float32(1.0 / math.factorial(12))
    for power, sign in ((10, -1.0), (8, 1.0), (6, -1.0), (4, 1.0), (2, -1.0), (0, 1.0)):
        cosine = cosine * square + jnp.float32(sign / math.factorial(power))
    return 2.0 * sine * cosine, 1.0 - 2.0 * sine * sine


def product(left, right, contract):
    dims = (contract, ((), ()))
    dot = functools.partial(
        lax.dot_general, dimension_numbers=dims, preferred_element_type=jnp.float32
    )
    return dot(left[0], right[0]) + (dot(left[0], right[1]) + dot(left[1], right[0]))


NN = ((1,), (0,))
NT = ((1,), (1,))


def partner(step):
    return lax.bitwise_xor(lax.axis_index("depth"), step)


def rows_with(step, rows):
    return pl.ds(pl.multiple_of(partner(step) * rows, rows), rows)


def refocus_kernel(pieces, table_ref, *refs):
    field_refs, phase_refs = refs[:pieces], refs[pieces : 2 * pieces]
    out_refs = refs[2 * pieces : 3 * pieces]
    left_ref, right_ref, *whole_refs = refs[3 * pieces :]
    extent = table_ref.shape[1]

    @pl.when(pl.program_id(0) == 0)
    def _():
        for part in range(2):
            cosine, sine = table_ref[part], table_ref[2 + part]
            left_ref[part, :extent, :extent] = cosine
            left_ref[part, :extent, extent:] = -sine
            left_ref[part, extent:, :extent] = sine
            left_ref[part, extent:, extent:] = cosine
            right_ref[part, :extent, :extent] = cosine
            right_ref[part, :extent, extent:] = sine
            right_ref[part, extent:, :extent] = -sine
            right_ref[part, extent:, extent:] = cosine

    left = (left_ref[0], left_ref[1])
    right = (right_ref[0], right_ref[1])

    def one(at, whole_ref):
        def whole(refs):
            if pieces == 1:
                return refs[0][:, at].reshape(extent, extent)
            for step, ref in enumerate(refs):
                whole_ref[rows_with(step, ref.shape[1]), :] = ref[at]
            return whole_ref[...]

        half_turned = product(
            (left_ref[0, :, :extent], left_ref[1, :, :extent]), split(whole(field_refs)), NT
        )
        half_turned = jnp.concatenate([half_turned[:extent], half_turned[extent:]], axis=1)
        spectrum = product(split(half_turned), right, NN)
        spec_real, spec_negated = spectrum[:, :extent], spectrum[:, extent:]
        sine, cosine = sincos(whole(phase_refs))
        prop_real = spec_real * cosine + spec_negated * sine
        prop_imag = spec_real * sine - spec_negated * cosine
        propagated = jnp.concatenate([prop_real, prop_imag], axis=1)
        back = product(left, split(propagated), NT)
        back = jnp.concatenate([back[:extent], back[extent:]], axis=1)
        field = product(split(back), right, NN)
        field_real, field_imag = field[:, :extent], field[:, extent:]
        power = field_real * field_real + field_imag * field_imag
        intensity = power * (1.0 / float(extent) ** 4)
        if pieces == 1:
            shape = out_refs[0].shape
            out_refs[0][:, at] = intensity.reshape(shape[:1] + shape[2:])
        else:
            whole_ref[...] = intensity
            for step, ref in enumerate(out_refs):
                ref[at] = whole_ref[rows_with(step, ref.shape[1]), :]

    for at, whole_ref in enumerate(whole_refs):
        one(at, whole_ref)


def refocus(fields, phases, chunk=0):
    pieces, extent = len(fields), fields[0].shape[-1]
    if pieces == 1:
        slots = fields[0].shape[1]
        together = math.gcd(slots, TOGETHER)

        def spec(array):
            block = array.shape[:1] + (together,) + array.shape[2:]
            return pl.BlockSpec(block, lambda i: (0, i, 0, 0))
    else:
        slots = phases[0].shape[0]
        together = math.gcd(slots, TOGETHER)

        def spec(array):
            first = chunk * slots // together if array.shape[0] > slots else 0
            return pl.BlockSpec((together,) + array.shape[1:], lambda i: (first + i, 0, 0))

    shape = fields[0].shape if pieces == 1 else (slots,) + fields[0].shape[1:]
    outs = [jax.ShapeDtypeStruct(shape, jnp.float32)] * pieces
    return pl.pallas_call(
        functools.partial(refocus_kernel, pieces),
        grid=(slots // together,),
        in_specs=[pl.BlockSpec((4, extent, extent), lambda i: (0, 0, 0))]
        + [spec(array) for array in [*fields, *phases]],
        out_specs=[spec(array) for array in outs],
        out_shape=outs,
        scratch_shapes=[pltpu.VMEM((2, 2 * extent, 2 * extent), jnp.bfloat16)] * 2
        + [pltpu.VMEM((extent, extent), jnp.float32)] * together,
        name="refocus",
    )(jnp.asarray(tables(extent)), *fields, *phases)


def move_kernel(scatter, filled, *refs):
    index_ref, source_ref, out_ref, held, come, gone = refs[0], refs[1], *refs[-4:]
    count = held.shape[0]

    def guarded(place, act):
        if filled:
            act()
        else:
            pl.when(place >= 0)(act)

    def each(act):
        def step(i, carry):
            guarded(index_ref[i], lambda: act(i))
            return carry

        lax.fori_loop(0, count, step, 0)

    def fetch(i):
        block = source_ref.at[i if scatter else index_ref[i]]
        return pltpu.make_async_copy(block, held.at[i], come.at[i])

    def store(i):
        block = out_ref.at[index_ref[i] if scatter else i]
        return pltpu.make_async_copy(held.at[i], block, gone.at[i])

    def pass_on(i):
        fetch(i).wait()
        store(i).start()

    each(lambda i: fetch(i).start())
    each(pass_on)
    each(lambda i: store(i).wait())


def move(index, source, out_shape, scatter, filled, into=None):
    count = index.shape[0]
    anywhere = pl.BlockSpec(memory_space=pl.ANY)
    operands = (source,) if into is None else (source, into)
    return pl.pallas_call(
        functools.partial(move_kernel, scatter, filled),
        grid_spec=pltpu.PrefetchScalarGridSpec(
            num_scalar_prefetch=1,
            in_specs=[anywhere] * len(operands),
            out_specs=anywhere,
            scratch_shapes=[
                pltpu.VMEM((count,) + source.shape[1:], source.dtype),
                pltpu.SemaphoreType.DMA((count,)),
                pltpu.SemaphoreType.DMA((count,)),
            ],
        ),
        out_shape=jax.ShapeDtypeStruct(out_shape, source.dtype),
        input_output_aliases={} if into is None else {2: 0},
        name="scatter_blocks" if scatter else "gather_blocks",
    )(index, *operands)


def loop(count, act):
    def step(i, carry):
        act(i)
        return carry

    lax.fori_loop(0, count, step, 0)


ANYWHERE = pl.BlockSpec(memory_space=pl.ANY)
SCALARS = pl.BlockSpec(memory_space=pltpu.SMEM)
LOCAL = pl.BlockSpec(memory_space=pltpu.VMEM)


def pieces_kernel(steps, patches_ref, *refs):
    out_refs, sems = refs[:-1], refs[-1]

    def copy(at, step):
        size = out_refs[at].shape[0]
        first = pl.multiple_of(partner(step) * size, size)
        return pltpu.make_async_copy(
            patches_ref.at[pl.ds(first, size)], out_refs[at], sems.at[at]
        )

    for at, step in enumerate(steps):
        copy(at, step).start()
    for at, step in enumerate(steps):
        copy(at, step).wait()


def pieces_of(patches, parts, steps, stay):
    shape = (patches.shape[0] // parts,) + patches.shape[1:]
    made = pltpu.VMEM if stay else jax.ShapeDtypeStruct
    return pl.pallas_call(
        functools.partial(pieces_kernel, steps),
        in_specs=[ANYWHERE],
        out_specs=[LOCAL] * len(steps),
        out_shape=[made(shape, patches.dtype)] * len(steps),
        scratch_shapes=[pltpu.SemaphoreType.DMA((len(steps),))],
        name="pieces",
    )(patches)


def table_kernel(filled, owner_ref, level_ref, slot_ref, wanted_ref, taken):
    owners, slot_count = taken.shape[0], wanted_ref.shape[0]

    def clear(i):
        taken[i] = 0

    loop(owners, clear)
    if not filled:

        def empty(i):
            wanted_ref[i] = 0

        loop(slot_count, empty)

    def place(i):
        owner = owner_ref[i]
        rank = taken[owner]
        taken[owner] = rank + 1
        slot = owner * (slot_count // owners) + rank
        slot_ref[i] = slot
        wanted_ref[slot] = level_ref[i]

    loop(owner_ref.shape[0], place)


def slot_table(owner, level, owners, slot_count):
    count = owner.shape[0]
    return pl.pallas_call(
        functools.partial(table_kernel, count == slot_count),
        in_specs=[SCALARS, SCALARS],
        out_specs=[SCALARS, SCALARS],
        out_shape=[
            jax.ShapeDtypeStruct((count,), jnp.int32),
            jax.ShapeDtypeStruct((slot_count,), jnp.int32),
        ],
        scratch_shapes=[pltpu.SMEM((owners,), jnp.int32)],
        name="slot_table",
    )(owner, level)


def order_kernel(chunk, chunks, slot_ref, source_ref, *refs):
    out_refs, (held, come, gone) = refs[:-3], refs[-3:]
    parts, size = held.shape[:2]

    def fetch(step):
        def one(i):
            slot = slot_ref[(partner(step) * chunks + chunk) * size + i]
            pltpu.make_async_copy(
                source_ref.at[slot], held.at[step, i], come.at[step, i]
            ).start()

        return one

    def pass_on(step):
        def one(i):
            pltpu.make_async_copy(source_ref.at[0], held.at[step, i], come.at[step, i]).wait()

        return one

    def store(step):
        return pltpu.make_async_copy(held.at[step], out_refs[step], gone.at[step])

    for step in range(parts):
        loop(size, fetch(step))
    for step in range(parts):
        loop(size, pass_on(step))
        store(step).start()
    for step in range(parts):
        store(step).wait()


def in_order(slots, source, parts, chunk, chunks):
    block = source.shape[1:]
    size = slots.shape[0] // (parts * chunks)
    return pl.pallas_call(
        functools.partial(order_kernel, chunk, chunks),
        in_specs=[SCALARS, ANYWHERE],
        out_specs=[ANYWHERE] * parts,
        out_shape=[jax.ShapeDtypeStruct((size,) + block, source.dtype)] * parts,
        scratch_shapes=[
            pltpu.VMEM((parts, size) + block, source.dtype),
            pltpu.SemaphoreType.DMA((parts, size)),
            pltpu.SemaphoreType.DMA((parts,)),
        ],
        name="in_order",
    )(slots, source)


def store_kernel(chunk, chunks, steps, *refs):
    source_refs, out_ref, gone = refs[: len(steps)], refs[-2], refs[-1]

    def copy(at, step):
        size = source_refs[at].shape[0]
        first = pl.multiple_of((partner(step) * chunks + chunk) * size, size)
        return pltpu.make_async_copy(source_refs[at], out_ref.at[pl.ds(first, size)], gone.at[at])

    for at, step in enumerate(steps):
        copy(at, step).start()
    for at, step in enumerate(steps):
        copy(at, step).wait()


def store(sources, into, out_shape, chunk, chunks, steps):
    sources = [pltpu.with_memory_space_constraint(source, pltpu.VMEM) for source in sources]
    operands = sources if into is None else sources + [into]
    return pl.pallas_call(
        functools.partial(store_kernel, chunk, chunks, steps),
        in_specs=[LOCAL] * len(sources) + [ANYWHERE] * (into is not None),
        out_specs=ANYWHERE,
        out_shape=jax.ShapeDtypeStruct(out_shape, jnp.float32),
        scratch_shapes=[pltpu.SemaphoreType.DMA((len(steps),))],
        input_output_aliases={} if into is None else {len(sources): 0},
        name="store",
    )(*operands)


def swap(arrays):
    parts = len(arrays)
    swapped = list(arrays)
    for step in range(parts - 1, 0, -1):
        swapped[step] = lax.ppermute(
            arrays[step], "depth", [(part, part ^ step) for part in range(parts)]
        )
    return swapped


def exchange(values, axes):
    return lax.all_to_all(values, axes, split_axis=0, concat_axis=0, tiled=True)


def by_patch(patches, patch_owner, patch_level, phases):
    owners, parts = lax.axis_size("tile"), lax.axis_size("depth")
    slot_count = owners * CAP
    (longest,) = pieces_of(patches, parts, (parts - 1,), True)
    slots, wanted = slot_table(patch_owner[:, 0], patch_level, owners, slot_count)
    wanted = exchange(wanted.reshape(owners, CAP), "tile").reshape(-1)
    rest = pieces_of(patches, parts, tuple(range(parts - 1)), False)
    fields = swap([*rest, longest])
    picked = move(wanted, phases, (slot_count,) + phases.shape[1:], False, True)
    arrived = exchange(picked, "tile")
    result = None
    for chunk in range(CHUNKS):
        chosen = in_order(slots, arrived, parts, chunk, CHUNKS)
        chosen = swap(chosen)
        local = refocus(fields, chosen, chunk)
        backs = swap(local)
        every = tuple(range(parts))
        last = chunk == CHUNKS - 1
        for steps in [(step,) for step in (*every[:2], *every[:1:-1])] if last else (every,):
            sources = [backs[step] for step in steps]
            result = store(sources, result, patches.shape, chunk, CHUNKS, steps)
    return result


def by_owner(patches, patch_owner, patch_level, phases):
    patch_count, row_count, extent = patches.shape
    owners, parts = lax.axis_size("tile"), lax.axis_size("depth")
    slot_count = owners * CAP
    filled = slot_count == patch_count
    owner = patch_owner[:, 0]
    numbers = jnp.arange(patch_count, dtype=jnp.int32)
    rank = jnp.sum(
        (owner[:, None] == owner[None, :]) & (numbers[None, :] < numbers[:, None]),
        axis=1,
        dtype=jnp.int32,
    )
    slot_hot = jnp.arange(slot_count, dtype=jnp.int32)[:, None] == (owner * CAP + rank)[None, :]
    wanted = jnp.sum(jnp.where(slot_hot, patch_level[None, :], 0), axis=1, dtype=jnp.int32)
    order = jnp.sum(jnp.where(slot_hot, numbers[None, :] + 1, 0), axis=1, dtype=jnp.int32) - 1
    wanted = exchange(wanted.reshape(owners, CAP), "tile").reshape(-1)
    field = exchange(move(order, patches, (slot_count,) + patches.shape[1:], False, filled), "depth")
    picked = move(wanted, phases, (slot_count,) + phases.shape[1:], False, True)
    phase = exchange(exchange(picked, "tile"), "depth")
    (local,) = refocus(
        [field.reshape(parts, -1, row_count, extent)],
        [phase.reshape((parts, -1) + phases.shape[1:])],
    )
    back = exchange(local.reshape(-1, row_count, extent), "depth")
    return move(order, back, patches.shape, True, filled)


def in_shares(parts):
    return parts in (2, 4)


def on_device(patches, patch_owner, patch_level, phases):
    turned = jnp.transpose(phases, (0, 2, 1))
    plan = by_patch if in_shares(lax.axis_size("depth")) else by_owner
    return plan(patches, patch_owner, patch_level, turned)


def solution(mesh):
    return jax.shard_map(
        on_device,
        mesh=mesh,
        in_specs=(P("tile", "depth", None), P("tile", None), P("tile"), P("tile", None, "depth")),
        out_specs=P("tile", "depth", None),
        check_vma=False,
    )
```

```python
import functools
import math

import jax
import jax.numpy as jnp
import numpy as np
from jax import lax
from jax.experimental import pallas as pl
from jax.experimental.pallas import tpu as pltpu
from jax.sharding import PartitionSpec as P


CAP = 8
CHUNKS = 2
TOGETHER = 2


def split(values):
    high = values.astype(jnp.bfloat16)
    low = (values - high.astype(jnp.float32)).astype(jnp.bfloat16)
    return high, low


def tables(extent):
    index = np.arange(extent)
    angles = (index[:, None] * index[None, :] % extent) * (2.0 * math.pi / extent)
    parts = []
    for table in (np.cos(angles), np.sin(angles)):
        table = table.astype(np.float32)
        high = table.astype(jnp.bfloat16)
        parts += [high, (table - high.astype(np.float32)).astype(jnp.bfloat16)]
    return np.stack(parts)


def sincos(angle):
    half = angle * 0.5
    square = half * half
    sine = jnp.float32(-1.0 / math.factorial(11))
    for power, sign in ((9, 1.0), (7, -1.0), (5, 1.0), (3, -1.0), (1, 1.0)):
        sine = sine * square + jnp.float32(sign / math.factorial(power))
    sine = sine * half
    cosine = jnp.float32(1.0 / math.factorial(12))
    for power, sign in ((10, -1.0), (8, 1.0), (6, -1.0), (4, 1.0), (2, -1.0), (0, 1.0)):
        cosine = cosine * square + jnp.float32(sign / math.factorial(power))
    return 2.0 * sine * cosine, 1.0 - 2.0 * sine * sine


def product(left, right, contract):
    dims = (contract, ((), ()))
    dot = functools.partial(
        lax.dot_general, dimension_numbers=dims, preferred_element_type=jnp.float32
    )
    return dot(left[0], right[0]) + (dot(left[0], right[1]) + dot(left[1], right[0]))


NN = ((1,), (0,))
NT = ((1,), (1,))


def partner(step):
    return lax.bitwise_xor(lax.axis_index("depth"), step)


def rows_with(step, rows):
    return pl.ds(pl.multiple_of(partner(step) * rows, rows), rows)


def refocus_kernel(pieces, table_ref, *refs):
    field_refs, phase_refs = refs[:pieces], refs[pieces : 2 * pieces]
    out_refs = refs[2 * pieces : 3 * pieces]
    left_ref, right_ref, *whole_refs = refs[3 * pieces :]
    extent = table_ref.shape[1]

    @pl.when(pl.program_id(0) == 0)
    def _():
        for part in range(2):
            cosine, sine = table_ref[part], table_ref[2 + part]
            left_ref[part, :extent, :extent] = cosine
            left_ref[part, :extent, extent:] = -sine
            left_ref[part, extent:, :extent] = sine
            left_ref[part, extent:, extent:] = cosine
            right_ref[part, :extent, :extent] = cosine
            right_ref[part, :extent, extent:] = sine
            right_ref[part, extent:, :extent] = -sine
            right_ref[part, extent:, extent:] = cosine

    left = (left_ref[0], left_ref[1])
    right = (right_ref[0], right_ref[1])

    def one(at, whole_ref):
        def whole(refs):
            if pieces == 1:
                return refs[0][:, at].reshape(extent, extent)
            for step, ref in enumerate(refs):
                whole_ref[rows_with(step, ref.shape[1]), :] = ref[at]
            return whole_ref[...]

        half_turned = product(
            (left_ref[0, :, :extent], left_ref[1, :, :extent]), split(whole(field_refs)), NT
        )
        half_turned = jnp.concatenate([half_turned[:extent], half_turned[extent:]], axis=1)
        spectrum = product(split(half_turned), right, NN)
        spec_real, spec_negated = spectrum[:, :extent], spectrum[:, extent:]
        sine, cosine = sincos(whole(phase_refs))
        prop_real = spec_real * cosine + spec_negated * sine
        prop_imag = spec_real * sine - spec_negated * cosine
        propagated = jnp.concatenate([prop_real, prop_imag], axis=1)
        back = product(left, split(propagated), NT)
        back = jnp.concatenate([back[:extent], back[extent:]], axis=1)
        field = product(split(back), right, NN)
        field_real, field_imag = field[:, :extent], field[:, extent:]
        power = field_real * field_real + field_imag * field_imag
        intensity = power * (1.0 / float(extent) ** 4)
        if pieces == 1:
            shape = out_refs[0].shape
            out_refs[0][:, at] = intensity.reshape(shape[:1] + shape[2:])
        else:
            whole_ref[...] = intensity
            for step, ref in enumerate(out_refs):
                ref[at] = whole_ref[rows_with(step, ref.shape[1]), :]

    for at, whole_ref in enumerate(whole_refs):
        one(at, whole_ref)


def refocus(fields, phases, chunk=0):
    pieces, extent = len(fields), fields[0].shape[-1]
    if pieces == 1:
        slots = fields[0].shape[1]
        together = math.gcd(slots, TOGETHER)

        def spec(array):
            block = array.shape[:1] + (together,) + array.shape[2:]
            return pl.BlockSpec(block, lambda i: (0, i, 0, 0))
    else:
        slots = phases[0].shape[0]
        together = math.gcd(slots, TOGETHER)

        def spec(array):
            first = chunk * slots // together if array.shape[0] > slots else 0
            return pl.BlockSpec((together,) + array.shape[1:], lambda i: (first + i, 0, 0))

    shape = fields[0].shape if pieces == 1 else (slots,) + fields[0].shape[1:]
    outs = [jax.ShapeDtypeStruct(shape, jnp.float32)] * pieces
    return pl.pallas_call(
        functools.partial(refocus_kernel, pieces),
        grid=(slots // together,),
        in_specs=[pl.BlockSpec((4, extent, extent), lambda i: (0, 0, 0))]
        + [spec(array) for array in [*fields, *phases]],
        out_specs=[spec(array) for array in outs],
        out_shape=outs,
        scratch_shapes=[pltpu.VMEM((2, 2 * extent, 2 * extent), jnp.bfloat16)] * 2
        + [pltpu.VMEM((extent, extent), jnp.float32)] * together,
        name="refocus",
    )(jnp.asarray(tables(extent)), *fields, *phases)


def move_kernel(scatter, filled, *refs):
    index_ref, source_ref, out_ref, held, come, gone = refs[0], refs[1], *refs[-4:]
    count = held.shape[0]

    def guarded(place, act):
        if filled:
            act()
        else:
            pl.when(place >= 0)(act)

    def each(act):
        def step(i, carry):
            guarded(index_ref[i], lambda: act(i))
            return carry

        lax.fori_loop(0, count, step, 0)

    def fetch(i):
        block = source_ref.at[i if scatter else index_ref[i]]
        return pltpu.make_async_copy(block, held.at[i], come.at[i])

    def store(i):
        block = out_ref.at[index_ref[i] if scatter else i]
        return pltpu.make_async_copy(held.at[i], block, gone.at[i])

    def pass_on(i):
        fetch(i).wait()
        store(i).start()

    each(lambda i: fetch(i).start())
    each(pass_on)
    each(lambda i: store(i).wait())


def move(index, source, out_shape, scatter, filled, into=None):
    count = index.shape[0]
    anywhere = pl.BlockSpec(memory_space=pl.ANY)
    operands = (source,) if into is None else (source, into)
    return pl.pallas_call(
        functools.partial(move_kernel, scatter, filled),
        grid_spec=pltpu.PrefetchScalarGridSpec(
            num_scalar_prefetch=1,
            in_specs=[anywhere] * len(operands),
            out_specs=anywhere,
            scratch_shapes=[
                pltpu.VMEM((count,) + source.shape[1:], source.dtype),
                pltpu.SemaphoreType.DMA((count,)),
                pltpu.SemaphoreType.DMA((count,)),
            ],
        ),
        out_shape=jax.ShapeDtypeStruct(out_shape, source.dtype),
        input_output_aliases={} if into is None else {2: 0},
        name="scatter_blocks" if scatter else "gather_blocks",
    )(index, *operands)


def loop(count, act):
    def step(i, carry):
        act(i)
        return carry

    lax.fori_loop(0, count, step, 0)


ANYWHERE = pl.BlockSpec(memory_space=pl.ANY)
SCALARS = pl.BlockSpec(memory_space=pltpu.SMEM)
LOCAL = pl.BlockSpec(memory_space=pltpu.VMEM)


def pieces_kernel(steps, patches_ref, *refs):
    out_refs, sems = refs[:-1], refs[-1]

    def copy(at, step):
        size = out_refs[at].shape[0]
        first = pl.multiple_of(partner(step) * size, size)
        return pltpu.make_async_copy(
            patches_ref.at[pl.ds(first, size)], out_refs[at], sems.at[at]
        )

    for at, step in enumerate(steps):
        copy(at, step).start()
    for at, step in enumerate(steps):
        copy(at, step).wait()


def pieces_of(patches, parts, steps, stay):
    shape = (patches.shape[0] // parts,) + patches.shape[1:]
    made = pltpu.VMEM if stay else jax.ShapeDtypeStruct
    return pl.pallas_call(
        functools.partial(pieces_kernel, steps),
        in_specs=[ANYWHERE],
        out_specs=[LOCAL] * len(steps),
        out_shape=[made(shape, patches.dtype)] * len(steps),
        scratch_shapes=[pltpu.SemaphoreType.DMA((len(steps),))],
        name="pieces",
    )(patches)


def table_kernel(filled, owner_ref, level_ref, slot_ref, wanted_ref, taken):
    owners, slot_count = taken.shape[0], wanted_ref.shape[0]

    def clear(i):
        taken[i] = 0

    loop(owners, clear)
    if not filled:

        def empty(i):
            wanted_ref[i] = 0

        loop(slot_count, empty)

    def place(i):
        owner = owner_ref[i]
        rank = taken[owner]
        taken[owner] = rank + 1
        slot = owner * (slot_count // owners) + rank
        slot_ref[i] = slot
        wanted_ref[slot] = level_ref[i]

    loop(owner_ref.shape[0], place)


def slot_table(owner, level, owners, slot_count):
    count = owner.shape[0]
    return pl.pallas_call(
        functools.partial(table_kernel, count == slot_count),
        in_specs=[SCALARS, SCALARS],
        out_specs=[SCALARS, SCALARS],
        out_shape=[
            jax.ShapeDtypeStruct((count,), jnp.int32),
            jax.ShapeDtypeStruct((slot_count,), jnp.int32),
        ],
        scratch_shapes=[pltpu.SMEM((owners,), jnp.int32)],
        name="slot_table",
    )(owner, level)


def order_kernel(chunk, chunks, slot_ref, source_ref, *refs):
    out_refs, (held, come, gone) = refs[:-3], refs[-3:]
    parts, size = held.shape[:2]

    def fetch(step):
        def one(i):
            slot = slot_ref[(partner(step) * chunks + chunk) * size + i]
            pltpu.make_async_copy(
                source_ref.at[slot], held.at[step, i], come.at[step, i]
            ).start()

        return one

    def pass_on(step):
        def one(i):
            pltpu.make_async_copy(source_ref.at[0], held.at[step, i], come.at[step, i]).wait()

        return one

    def store(step):
        return pltpu.make_async_copy(held.at[step], out_refs[step], gone.at[step])

    for step in range(parts):
        loop(size, fetch(step))
    for step in range(parts):
        loop(size, pass_on(step))
        store(step).start()
    for step in range(parts):
        store(step).wait()


def in_order(slots, source, parts, chunk, chunks):
    block = source.shape[1:]
    size = slots.shape[0] // (parts * chunks)
    return pl.pallas_call(
        functools.partial(order_kernel, chunk, chunks),
        in_specs=[SCALARS, ANYWHERE],
        out_specs=[ANYWHERE] * parts,
        out_shape=[jax.ShapeDtypeStruct((size,) + block, source.dtype)] * parts,
        scratch_shapes=[
            pltpu.VMEM((parts, size) + block, source.dtype),
            pltpu.SemaphoreType.DMA((parts, size)),
            pltpu.SemaphoreType.DMA((parts,)),
        ],
        name="in_order",
    )(slots, source)


def store_kernel(chunk, chunks, steps, offset, *refs):
    source_refs, out_ref, gone = refs[: len(steps)], refs[-2], refs[-1]

    def copy(at, step):
        size = source_refs[at].shape[0]
        share = out_ref.shape[0] // (lax.axis_size("depth") * chunks)
        first = (partner(step) * chunks + chunk) * share + offset
        return pltpu.make_async_copy(source_refs[at], out_ref.at[pl.ds(first, size)], gone.at[at])

    for at, step in enumerate(steps):
        copy(at, step).start()
    for at, step in enumerate(steps):
        copy(at, step).wait()


def store(sources, into, out_shape, chunk, chunks, steps, offset=0):
    sources = [pltpu.with_memory_space_constraint(source, pltpu.VMEM) for source in sources]
    operands = sources if into is None else sources + [into]
    return pl.pallas_call(
        functools.partial(store_kernel, chunk, chunks, steps, offset),
        in_specs=[LOCAL] * len(sources) + [ANYWHERE] * (into is not None),
        out_specs=ANYWHERE,
        out_shape=jax.ShapeDtypeStruct(out_shape, jnp.float32),
        scratch_shapes=[pltpu.SemaphoreType.DMA((len(steps),))],
        input_output_aliases={} if into is None else {len(sources): 0},
        name="store",
    )(*operands)


def swap(arrays, halves=False):
    parts = len(arrays)
    swapped = list(arrays)
    for step in range(parts - 1, 0, -1):
        pairs = [(part, part ^ step) for part in range(parts)]
        if halves and step == 2:
            swapped[step] = [
                lax.ppermute(half, "depth", pairs) for half in jnp.split(arrays[step], 2)
            ]
        else:
            swapped[step] = lax.ppermute(arrays[step], "depth", pairs)
    return swapped


def exchange(values, axes):
    return lax.all_to_all(values, axes, split_axis=0, concat_axis=0, tiled=True)


def by_patch(patches, patch_owner, patch_level, phases):
    owners, parts = lax.axis_size("tile"), lax.axis_size("depth")
    slot_count = owners * CAP
    (longest,) = pieces_of(patches, parts, (parts - 1,), True)
    slots, wanted = slot_table(patch_owner[:, 0], patch_level, owners, slot_count)
    wanted = exchange(wanted.reshape(owners, CAP), "tile").reshape(-1)
    rest = pieces_of(patches, parts, tuple(range(parts - 1)), False)
    fields = swap([*rest, longest])
    picked = move(wanted, phases, (slot_count,) + phases.shape[1:], False, True)
    arrived = exchange(picked, "tile")
    result = None
    for chunk in range(CHUNKS):
        chosen = in_order(slots, arrived, parts, chunk, CHUNKS)
        chosen = swap(chosen)
        local = refocus(fields, chosen, chunk)
        backs = swap(local, chunk == CHUNKS - 1)
        every = tuple(range(parts))
        last = chunk == CHUNKS - 1
        if not last:
            result = store(backs, result, patches.shape, chunk, CHUNKS, every)
            continue
        for step in (*every[:2], *every[:1:-1]):
            first = 0
            for source in jax.tree.leaves(backs[step]):
                result = store([source], result, patches.shape, chunk, CHUNKS, (step,), first)
                first += source.shape[0]
    return result


def by_owner(patches, patch_owner, patch_level, phases):
    patch_count, row_count, extent = patches.shape
    owners, parts = lax.axis_size("tile"), lax.axis_size("depth")
    slot_count = owners * CAP
    filled = slot_count == patch_count
    owner = patch_owner[:, 0]
    numbers = jnp.arange(patch_count, dtype=jnp.int32)
    rank = jnp.sum(
        (owner[:, None] == owner[None, :]) & (numbers[None, :] < numbers[:, None]),
        axis=1,
        dtype=jnp.int32,
    )
    slot_hot = jnp.arange(slot_count, dtype=jnp.int32)[:, None] == (owner * CAP + rank)[None, :]
    wanted = jnp.sum(jnp.where(slot_hot, patch_level[None, :], 0), axis=1, dtype=jnp.int32)
    order = jnp.sum(jnp.where(slot_hot, numbers[None, :] + 1, 0), axis=1, dtype=jnp.int32) - 1
    wanted = exchange(wanted.reshape(owners, CAP), "tile").reshape(-1)
    field = exchange(move(order, patches, (slot_count,) + patches.shape[1:], False, filled), "depth")
    picked = move(wanted, phases, (slot_count,) + phases.shape[1:], False, True)
    phase = exchange(exchange(picked, "tile"), "depth")
    (local,) = refocus(
        [field.reshape(parts, -1, row_count, extent)],
        [phase.reshape((parts, -1) + phases.shape[1:])],
    )
    back = exchange(local.reshape(-1, row_count, extent), "depth")
    return move(order, back, patches.shape, True, filled)


def in_shares(parts):
    return parts in (2, 4)


def on_device(patches, patch_owner, patch_level, phases):
    turned = jnp.transpose(phases, (0, 2, 1))
    plan = by_patch if in_shares(lax.axis_size("depth")) else by_owner
    return plan(patches, patch_owner, patch_level, turned)


def solution(mesh):
    return jax.shard_map(
        on_device,
        mesh=mesh,
        in_specs=(P("tile", "depth", None), P("tile", None), P("tile"), P("tile", None, "depth")),
        out_specs=P("tile", "depth", None),
        check_vma=False,
    )
```
